32 devices in a mesh: blk: 2 (over y), sector: 16 (over z, x, core).
Axes of the slice: x: 2, y: 2, z: 4, core: 2. Of those that a mesh axis runs over, the one named last changes fastest.
Arguments:
- state: float32 [5, 6, 6, 6, 4096], P(None, None, None, None, ('blk', 'sector')), may hold values from -6 to 6
- mean_flow: float32 [2, 4], replicated, may hold values from 0.2 to 1
- sector_offset: int32 [2], replicated, may hold values from 0 to 15
- frac_index: int32 [2], replicated, may hold values from 0 to 31
Outputs:
- new_state: float32 [5, 6, 6, 6, 4096], P(None, None, None, None, ('blk', 'sector'))
The draws below stay inside these ranges and needn't reach their ends.
All inputs are finite; a program needn't handle non-finite values.
Results may differ from the reference program's by a relative error of at most 0.0003.
Values sent between devices are 32-bit elements; how exact they have to be, the bound alone decides.
A program may use at most 192 MiB of HBM per device.

```python
import math
import jax
import jax.numpy as jnp
import numpy as np
from jax import lax

VARS = 5
NODES = 6
FRACS = 4
SECTIONS = 2
EA = 8
ER = 4
EZ = 4
CELLS = 4096
N_SECTOR = 16


def steps_of(stream_key, extent, shards, low, top_value):
    loudness = 1.0
    for axis_at, shards_of in shards:
        steps = jax.random.uniform(jax.random.fold_in(jax.random.fold_in(stream_key, 6), axis_at), (shards_of,), jnp.float32, low / len(shards), top_value / len(shards))
        loudness = loudness * jnp.repeat(jnp.exp(steps), extent[axis_at] // shards_of).reshape((-1,) + (1,) * (len(extent) - 1 - axis_at))
    return loudness


def bell_draw(stream_key, shape, deviation, bound, cuts=(), kind=jnp.bfloat16):
    factor_of = steps_of(stream_key, shape, cuts, -0.22, 0.18) if cuts else 1.0
    result = jax.random.normal(stream_key, shape, jnp.float32) * deviation * factor_of
    return jnp.minimum(jnp.maximum(result, -bound), bound).astype(kind)


def setup_inputs(seed: int = 0) -> dict:
    arg_keys = jax.random.split(jax.random.key(seed), 5)
    state = bell_draw(arg_keys[0], (VARS, NODES, NODES, NODES, CELLS), 1.0, 6.0, ((4, 32),), jnp.float32)
    mean_flow = jnp.clip(jax.random.uniform(arg_keys[1], (2, 4), jnp.float32, 0.2, 1.0), 0.2, 1.0)
    sector_offset = jax.random.randint(arg_keys[2], (SECTIONS,), 0, N_SECTOR).astype(jnp.int32)
    frac_index = jax.random.randint(arg_keys[3], (SECTIONS,), 0, EA * FRACS).astype(jnp.int32)
    return {"state": state, "mean_flow": mean_flow, "sector_offset": sector_offset, "frac_index": frac_index}


HIGHEST = lax.Precision.HIGHEST
TIME_STEP = 0.02

def lobatto_points(number):
    outer = math.sqrt(1.0 / 3.0 + 2.0 * math.sqrt(7.0) / 21.0)
    inner = math.sqrt(1.0 / 3.0 - 2.0 * math.sqrt(7.0) / 21.0)
    return np.array([-1.0, -outer, -inner, inner, outer, 1.0])

def derivative_matrix(points):
    number = points.shape[0]
    barycentric = np.array([1.0 / np.prod([points[column] - points[another] for another in range(number) if another != column]) for column in range(number)])
    matrix = np.zeros((number, number))
    for target in range(number):
        for source in range(number):
            if target != source:
                matrix[target, source] = barycentric[source] / barycentric[target] / (points[target] - points[source])
        matrix[target, target] = -np.sum(matrix[target])
    return matrix

def lagrange_weights(points, where_at):
    number = points.shape[0]
    columns = []
    for source in range(number):
        weight = jnp.ones_like(where_at)
        for another in range(number):
            if another != source:
                weight = weight * (where_at - points[another]) / (points[source] - points[another])
        columns.append(weight)
    return jnp.stack(columns, axis=1)

def mortar_tables(points, fraction):
    scaled = jnp.asarray((points + 1.0) / 2.0, jnp.float32)
    stator_upper = scaled > fraction
    stator_local = jnp.where(stator_upper, scaled - fraction, scaled - fraction + 1.0) * 2.0 - 1.0
    rotor_upper = scaled + fraction >= 1.0
    rotor_local = jnp.where(rotor_upper, scaled + fraction - 1.0, scaled + fraction) * 2.0 - 1.0
    return (stator_upper, lagrange_weights(points, stator_local), rotor_upper, lagrange_weights(points, rotor_local))

def mortar_values(lower_pick, upper_pick, choose_upper, weights):
    lower_value = jnp.einsum('ts,vrsRE->vrtRE', weights, lower_pick, precision=HIGHEST)
    upper_value = jnp.einsum('ts,vrsRE->vrtRE', weights, upper_pick, precision=HIGHEST)
    return jnp.where(choose_upper[None, None, :, None, None], upper_value, lower_value)

def flux_along(quantity, flow_row, direction):
    along_speed = flow_row[direction - 1]
    sound_speed = flow_row[3]
    pieces = [along_speed * quantity[member] for member in range(quantity.shape[0])]
    pieces[0] = pieces[0] + sound_speed * quantity[direction]
    pieces[direction] = pieces[direction] + sound_speed * quantity[0]
    return jnp.stack(pieces)

def face_jump(inside, outside, flow_inside, flow_outside, direction, normal, spread):
    flux_gap = flux_along(outside, flow_outside, direction) - flux_along(inside, flow_inside, direction)
    return 0.5 * normal * flux_gap - 0.5 * spread * (outside - inside)

def interface_correction(inside, outside, flow_inside, flow_outside, normal, spread, lift_factor):
    return -lift_factor * 2.0 * face_jump(inside, outside, flow_inside, flow_outside, 3, normal, spread)

def local_rate(current, flow_row, spreads, west_faces, east_faces, interface_term, is_rotor):
    number = current.shape[1]
    points = lobatto_points(number)
    derivative_table = jnp.asarray(derivative_matrix(points), jnp.float32)
    lift_factor = number * (number - 1) / 2.0
    elements = current.shape[-1]
    slab_size = EA * ER
    element_index = jnp.arange(elements, dtype=jnp.int32)
    azimuth_slot = element_index % EA
    radial_slot = element_index // EA % ER
    axial_slot = element_index // slab_size
    radius = 1.0 + (radial_slot.astype(jnp.float32) + 0.5) / ER
    azimuth_scale = 2.0 / radius
    rate_sum = -(azimuth_scale * jnp.einsum('ij,vzrjE->vzriE', derivative_table, flux_along(current, flow_row, 1), precision=HIGHEST))
    rate_sum = rate_sum - 2.0 * jnp.einsum('ij,vzjaE->vziaE', derivative_table, flux_along(current, flow_row, 2), precision=HIGHEST)
    rate_sum = rate_sum - 2.0 * jnp.einsum('ij,vjraE->viraE', derivative_table, flux_along(current, flow_row, 3), precision=HIGHEST)
    left_face = current[:, :, :, 0, :]
    right_face = current[:, :, :, -1, :]
    edge_zero = jnp.zeros(left_face.shape[:-1] + (1,), current.dtype)
    outside_left = jnp.where(azimuth_slot == 0, jnp.repeat(west_faces, EA, axis=-1), jnp.concatenate([edge_zero, right_face[..., :-1]], axis=-1))
    outside_right = jnp.where(azimuth_slot == EA - 1, jnp.repeat(east_faces, EA, axis=-1), jnp.concatenate([left_face[..., 1:], edge_zero], axis=-1))
    rate_sum = rate_sum.at[:, :, :, 0, :].add(-lift_factor * azimuth_scale * face_jump(left_face, outside_left, flow_row, flow_row, 1, -1.0, spreads[0]))
    rate_sum = rate_sum.at[:, :, :, -1, :].add(-lift_factor * azimuth_scale * face_jump(right_face, outside_right, flow_row, flow_row, 1, 1.0, spreads[0]))
    wall_flip = jnp.asarray([1.0, 1.0, -1.0, 1.0, 1.0], current.dtype)[:, None, None, None]
    lower_face = current[:, :, 0, :, :]
    upper_face = current[:, :, -1, :, :]
    cycle_zero = jnp.zeros(lower_face.shape[:-1] + (EA,), current.dtype)
    outside_lower = jnp.where(radial_slot == 0, wall_flip * lower_face, jnp.concatenate([cycle_zero, upper_face[..., :-EA]], axis=-1))
    outside_upper = jnp.where(radial_slot == ER - 1, wall_flip * upper_face, jnp.concatenate([lower_face[..., EA:], cycle_zero], axis=-1))
    rate_sum = rate_sum.at[:, :, 0, :, :].add(-lift_factor * 2.0 * face_jump(lower_face, outside_lower, flow_row, flow_row, 2, -1.0, spreads[1]))
    rate_sum = rate_sum.at[:, :, -1, :, :].add(-lift_factor * 2.0 * face_jump(upper_face, outside_upper, flow_row, flow_row, 2, 1.0, spreads[1]))
    bottom_face = current[:, 0]
    top_face = current[:, -1]
    slab_zero = jnp.zeros(bottom_face.shape[:-1] + (slab_size,), current.dtype)
    outside_bottom = jnp.concatenate([slab_zero, top_face[..., :-slab_size]], axis=-1)
    outside_top = jnp.concatenate([bottom_face[..., slab_size:], slab_zero], axis=-1)
    bottom_term = -lift_factor * 2.0 * face_jump(bottom_face, outside_bottom, flow_row, flow_row, 3, -1.0, spreads[2])
    top_term = -lift_factor * 2.0 * face_jump(top_face, outside_top, flow_row, flow_row, 3, 1.0, spreads[2])
    rate_sum = rate_sum.at[:, 0].add(jnp.where((axial_slot == 0) & jnp.logical_not(is_rotor), 0.0, bottom_term))
    rate_sum = rate_sum.at[:, -1].add(jnp.where((axial_slot == EZ - 1) & is_rotor, 0.0, top_term))
    zero_term = jnp.zeros_like(interface_term)
    rate_sum = rate_sum.at[:, 0, :, :, :slab_size].add(jnp.where(is_rotor, zero_term, interface_term))
    rate_sum = rate_sum.at[:, -1, :, :, elements - slab_size:].add(jnp.where(is_rotor, interface_term, zero_term))
    return rate_sum

def to_cycle(traces):
    shaped = traces.reshape(N_SECTOR, VARS, NODES, NODES, ER, EA)
    return jnp.transpose(shaped, (1, 2, 3, 4, 0, 5)).reshape(VARS, NODES, NODES, ER, N_SECTOR * EA)

def from_cycle(traces):
    shaped = traces.reshape(VARS, NODES, NODES, ER, N_SECTOR, EA)
    return jnp.transpose(shaped, (4, 0, 1, 2, 3, 5)).reshape(N_SECTOR, VARS, NODES, NODES, ER * EA)

def reference(state, mean_flow, sector_offset, frac_index):
    elements = EA * ER * EZ
    slab_size = EA * ER
    points = lobatto_points(NODES)
    lift_factor = NODES * (NODES - 1) / 2.0
    spreads = lax.optimization_barrier(jnp.max(jnp.abs(mean_flow[:, :3]), axis=0)) + jnp.max(mean_flow[:, 3])
    row_ids = jnp.repeat(jnp.arange(2, dtype=jnp.int32), N_SECTOR)

    def section_rate(current, section_index):
        blocks = jnp.moveaxis(current.reshape(VARS, NODES, NODES, NODES, 2, N_SECTOR, elements), (4, 5), (0, 1))
        right_edge = blocks[:, :, :, :, :, -1, EA - 1::EA]
        left_edge = blocks[:, :, :, :, :, 0, 0::EA]
        west_all = jnp.roll(right_edge, 1, axis=1)
        east_all = jnp.roll(left_edge, -1, axis=1)
        rotor_cycle = to_cycle(blocks[0, :, :, -1, :, :, elements - slab_size:])
        stator_cycle = to_cycle(blocks[1, :, :, 0, :, :, :slab_size])
        whole_steps = frac_index[section_index] // FRACS
        fraction = (frac_index[section_index] % FRACS).astype(jnp.float32) / FRACS
        shift_total = sector_offset[section_index] * EA + whole_steps
        stator_upper, stator_weights, rotor_upper, rotor_weights = mortar_tables(points, fraction)
        stator_plus = mortar_values(jnp.roll(rotor_cycle, shift_total + 1, axis=4), jnp.roll(rotor_cycle, shift_total, axis=4), stator_upper, stator_weights)
        stator_term = interface_correction(stator_cycle, stator_plus, mean_flow[1], mean_flow[0], -1.0, spreads[2], lift_factor)
        rotor_plus = mortar_values(jnp.roll(stator_cycle, -shift_total, axis=4), jnp.roll(stator_cycle, -shift_total - 1, axis=4), rotor_upper, rotor_weights)
        rotor_term = interface_correction(rotor_cycle, rotor_plus, mean_flow[0], mean_flow[1], 1.0, spreads[2], lift_factor)
        interface_all = jnp.stack([from_cycle(rotor_term), from_cycle(stator_term)])

        def block_rate(packed):
            block_state, west_faces, east_faces, interface_term, row_id = packed
            return local_rate(block_state, mean_flow[row_id], spreads, west_faces, east_faces, interface_term, row_id == 0)
        rates = lax.map(block_rate, (blocks.reshape((2 * N_SECTOR,) + blocks.shape[2:]), west_all.reshape((2 * N_SECTOR,) + west_all.shape[2:]), east_all.reshape((2 * N_SECTOR,) + east_all.shape[2:]), interface_all.reshape((2 * N_SECTOR,) + interface_all.shape[2:]), row_ids))
        rates = rates.reshape((2, N_SECTOR) + rates.shape[1:])
        return jnp.moveaxis(rates, (0, 1), (4, 5)).reshape(current.shape)
    middle = state + TIME_STEP * section_rate(state, 0)
    return 0.5 * state + 0.5 * (middle + TIME_STEP * section_rate(middle, 1))
```

```python
import functools
import math

import jax
import jax.numpy as jnp
import numpy as np
from jax import lax
from jax.experimental import pallas as pl
from jax.experimental.pallas import tpu as pltpu
from jax.sharding import PartitionSpec as P

FRACS = 4
EA = 8
ER = 4
EZ = 4
TIME_STEP = 0.02
V = 5
N = 6
LANES = 128
SLAB = EA * ER
TRACE_ROWS = 48
f32 = jnp.float32
MESH = pl.DeviceIdType.MESH


def lobatto_points():
    outer = math.sqrt(1.0 / 3.0 + 2.0 * math.sqrt(7.0) / 21.0)
    inner = math.sqrt(1.0 / 3.0 - 2.0 * math.sqrt(7.0) / 21.0)
    return np.array([-1.0, -outer, -inner, inner, outer, 1.0])


def derivative_matrix(points):
    number = points.shape[0]
    bary = np.array(
        [
            1.0 / np.prod([points[c] - points[o] for o in range(number) if o != c])
            for c in range(number)
        ]
    )
    matrix = np.zeros((number, number))
    for t in range(number):
        for s in range(number):
            if t != s:
                matrix[t, s] = bary[s] / bary[t] / (points[t] - points[s])
    return matrix


POINTS = lobatto_points()
DMAT = derivative_matrix(POINTS)
LIFT = N * (N - 1) / 2.0
HALF = 0.5 * LIFT


def stages_of(count):
    digits = []
    left = count
    while left > 1:
        radix = 4 if left % 4 == 0 else 2
        left //= radix
        digits.append((left, radix))
    return digits


def roll(x, by):
    by = by % LANES
    return x if by == 0 else pltpu.roll(x, by, 1)


def tile(v, a, b):
    return pl.multiple_of(((v * N + a) * N + b) * 8, 8)


def get(ref, v, a, b):
    return ref[pl.ds(tile(v, a, b), 8), :]


def choose(digit, options):
    out = options[0]
    for k in range(1, len(options)):
        out = jnp.where(digit == k, options[k], out)
    return out


def face(v, a, c):
    return pl.ds((v * N + a) * N * 8 + c, N, stride=8)


def by_sublane(values, rows):
    index = lax.broadcasted_iota(jnp.int32, (rows, LANES), 0)
    out = jnp.zeros((rows, LANES), f32)
    for k, value in enumerate(values):
        out = jnp.where(index == k, f32(value), out)
    return out


def kernel(
    sectors,
    flow_ref,
    offset_ref,
    frac_ref,
    dtab_ref,
    state_ref,
    out_ref,
    u_ref,
    w_ref,
    west_out,
    east_out,
    west_in,
    east_in,
    trace_out,
    hop_in,
    pair_in,
    send_sem,
    recv_sem,
):
    stages = stages_of(sectors)
    row = lax.axis_index("blk")
    me = lax.axis_index("sector")
    is_rotor = row == 0
    last_radix = stages[-1][1]

    def at(flip, off):
        return (1 - row if flip else row, lax.rem(me + off + sectors, sectors))

    targets = [(0, -1)]
    for s, (stride, radix) in enumerate(stages):
        flip = 1 if s == 0 else 0
        span = range(radix) if s == 0 else range(1, radix)
        if s == len(stages) - 1:
            span = range(1, radix + 1)
        for h in span:
            if (flip, h * stride) not in targets:
                targets.append((flip, h * stride))
    barrier = pltpu.get_barrier_semaphore()
    for flip, off in targets:
        pl.semaphore_signal(barrier, inc=1, device_id=at(flip, -off), device_id_type=MESH)

    lane = lax.broadcasted_iota(jnp.int32, (8, LANES), 1)
    lane6 = lane[:N]
    slot6 = lane6 % EA
    radial = (lane // EA) % ER
    s1 = 2.0 / (1.0 + (radial.astype(f32) + 0.5) / ER)
    s1_6 = s1[:N]

    def pick(k):
        return jnp.where(is_rotor, flow_ref[0, k], flow_ref[1, k])

    speed = [pick(k) for k in range(3)]
    sound = pick(3)
    other_axial = jnp.where(is_rotor, flow_ref[1, 2], flow_ref[0, 2])
    other_sound = jnp.where(is_rotor, flow_ref[1, 3], flow_ref[0, 3])
    top_sound = jnp.maximum(flow_ref[0, 3], flow_ref[1, 3])
    spread = [
        jnp.maximum(jnp.abs(flow_ref[0, k]), jnp.abs(flow_ref[1, k])) + top_sound for k in range(3)
    ]
    dcols = [by_sublane(DMAT[:, j], 8) for j in range(N)]
    own_a = jnp.where(is_rotor, N - 1, 0)

    def load_state(a, carry):
        for v in range(V):
            for b in range(N):
                u_ref[pl.ds(tile(v, a, b), N), :] = state_ref[v, a, b]
        return carry

    lax.fori_loop(0, N, load_state, 0)

    def pack(ref):
        for v in range(V):
            left = jnp.zeros((N, LANES), f32)
            right = jnp.zeros((N, LANES), f32)
            for a in range(N):
                left = jnp.where(slot6 == a, roll(ref[face(v, a, 0), :], a), left)
                right = jnp.where(slot6 == a, roll(ref[face(v, a, N - 1), :], a - EA + 1), right)
            west_out[v, pl.ds(0, N), :] = left
            east_out[v, pl.ds(0, N), :] = right
        quarter = lane6 // SLAB
        turned = jnp.where(is_rotor, (quarter + 1) % 4, quarter)
        for t in range(8):
            merged = jnp.zeros((N, LANES), f32)
            for q in range(4):
                n = 4 * t + q
                if n < V * N:
                    here = ref[pl.ds(tile(n // N, own_a, n % N), N), :]
                    merged = jnp.where(turned == q, roll(here, SLAB * q), merged)
            trace_out[pl.ds(N * t, N), :] = jnp.where(is_rotor, roll(merged, SLAB), merged)

    def copy(section, k, src, dst, target):
        return pltpu.make_async_remote_copy(
            src_ref=src,
            dst_ref=dst,
            send_sem=send_sem.at[section, k],
            recv_sem=recv_sem.at[section, k],
            device_id=target,
            device_id_type=MESH,
        )

    def send_first(section):
        copies = [
            copy(section, 2 + h, trace_out, hop_in.at[section, 0, h], at(1, h * stages[0][0]))
            for h in range(stages[0][1])
        ]
        halos = [
            copy(section, 0, west_out, west_in.at[section], at(0, -1)),
            copy(section, 1, east_out, east_in.at[section], at(0, 1)),
        ]
        for c in copies + halos:
            c.start()
        return copies, halos

    def forward(section, copies):
        amount = jnp.where(
            is_rotor,
            lax.rem(2 * sectors - offset_ref[section] - 1, sectors),
            lax.rem(offset_ref[section], sectors),
        )
        sem = 2 + stages[0][1]
        for s in range(1, len(stages)):
            for c in copies:
                c.wait()
            stride_before, radix_before = stages[s - 1]
            digit = lax.rem(amount // stride_before, radix_before)
            chosen = choose(digit, [hop_in[section, s - 1, h] for h in range(radix_before)])
            stride, radix = stages[s]
            if s == len(stages) - 1:
                dst, span = pair_in.at[section], range(1, radix + 1)
            else:
                dst, span = hop_in.at[section, s], range(1, radix)
            dst[0] = chosen
            copies = []
            for h in span:
                copies.append(copy(section, sem, dst.at[0], dst.at[h], at(0, h * stride)))
                sem += 1
            for c in copies:
                c.start()
        return copies, lax.rem(amount, last_radix)

    def volume(src, dst, base, scale):
        k1 = -scale * s1 * speed[0]
        c1 = -scale * s1 * sound
        k2 = jnp.full((8, LANES), -2.0 * scale * speed[1], f32)
        k3 = jnp.full((8, LANES), -2.0 * scale * speed[2], f32)
        c2 = jnp.full((8, LANES), -2.0 * scale * sound, f32)

        def at_b(b, carry):
            row_b = [dtab_ref[b, j] for j in range(N)]
            for a in range(N):
                kept = {}
                zero_sum = None
                for v in range(V):
                    start = tile(v, a, b)
                    g1 = dcols[0] * src[pl.ds(start, 1), :]
                    for j in range(1, N):
                        g1 = g1 + dcols[j] * src[pl.ds(start + j, 1), :]
                    g2 = row_b[0] * get(src, v, a, 0)
                    for j in range(1, N):
                        g2 = g2 + row_b[j] * get(src, v, a, j)
                    g3 = None
                    for j in range(N):
                        if j != a:
                            term = f32(DMAT[a, j]) * get(src, v, j, b)
                            g3 = term if g3 is None else g3 + term
                    total = base(v, a, b) + k1 * g1 + k2 * g2 + k3 * g3
                    if v == 0:
                        kept = {1: g1, 2: g2, 3: g3}
                        zero_sum = total
                        continue
                    if v == 1:
                        total = total + c1 * kept[1]
                        zero_sum = zero_sum + c1 * g1
                    if v == 2:
                        total = total + c2 * kept[2]
                        zero_sum = zero_sum + c2 * g2
                    if v == 3:
                        total = total + c2 * kept[3]
                        zero_sum = zero_sum + c2 * g3
                    dst[pl.ds(start, 8), :] = total
                dst[pl.ds(tile(0, a, b), 8), :] = zero_sum
            return carry

        lax.fori_loop(0, N, at_b, 0)

    def jumps(outside, inside, direction, sign, factor, along, acoustic):
        result = []
        for v in range(V):
            flux = along * outside[v]
            if v == 0:
                flux = flux + acoustic * outside[direction]
            if v == direction:
                flux = flux + acoustic * outside[0]
            gap = outside[v] if inside is None else outside[v] - inside[v]
            result.append(factor * (sign * flux + spread[direction - 1] * gap))
        return result

    def inner_faces(src, dst, scale):
        def azimuthal(a, carry):
            lows = [src[face(v, a, 0), :] for v in range(V)]
            highs = [src[face(v, a, N - 1), :] for v in range(V)]
            before = [jnp.where(slot6 == 0, 0.0, roll(x, 1)) for x in highs]
            after = [jnp.where(slot6 == EA - 1, 0.0, roll(x, -1)) for x in lows]
            factor = scale * HALF * s1_6
            for c, out, ins, sign in ((0, before, lows, 1.0), (N - 1, after, highs, -1.0)):
                for v, x in enumerate(jumps(out, ins, 1, sign, factor, speed[0], sound)):
                    dst[face(v, a, c), :] = dst[face(v, a, c), :] + x
            return carry

        lax.fori_loop(0, N, azimuthal, 0)

        def radial_faces(a, carry):
            lows = [get(src, v, a, 0) for v in range(V)]
            highs = [get(src, v, a, N - 1) for v in range(V)]
            below = [
                jnp.where(radial == 0, -lows[v] if v == 2 else lows[v], roll(highs[v], EA))
                for v in range(V)
            ]
            above = [
                jnp.where(radial == ER - 1, -highs[v] if v == 2 else highs[v], roll(lows[v], -EA))
                for v in range(V)
            ]
            factor = scale * LIFT
            for b, out, ins, sign in ((0, below, lows, 1.0), (N - 1, above, highs, -1.0)):
                for v, x in enumerate(jumps(out, ins, 2, sign, factor, speed[1], sound)):
                    dst[pl.ds(tile(v, a, b), 8), :] = get(dst, v, a, b) + x
            return carry

        lax.fori_loop(0, N, radial_faces, 0)

        def axial_faces(b, carry):
            lows = [get(src, v, 0, b) for v in range(V)]
            highs = [get(src, v, N - 1, b) for v in range(V)]
            below = [jnp.where(lane < SLAB, 0.0, roll(x, SLAB)) for x in highs]
            above = [jnp.where(lane >= LANES - SLAB, 0.0, roll(x, -SLAB)) for x in lows]
            factor = scale * LIFT
            for a, out, ins, sign in ((0, below, lows, 1.0), (N - 1, above, highs, -1.0)):
                for v, x in enumerate(jumps(out, ins, 3, sign, factor, speed[2], sound)):
                    dst[pl.ds(tile(v, a, b), 8), :] = get(dst, v, a, b) + x
            return carry

        lax.fori_loop(0, N, axial_faces, 0)

    def halo_faces(section, dst, scale):
        factor = scale * HALF * s1_6
        from_west = [east_in[section, v, pl.ds(0, N), :] for v in range(V)]
        from_east = [west_in[section, v, pl.ds(0, N), :] for v in range(V)]
        low = jumps(from_west, None, 1, 1.0, factor, speed[0], sound)
        high = jumps(from_east, None, 1, -1.0, factor, speed[0], sound)
        for v in range(V):
            for a in range(N):
                x = jnp.where(slot6 == 0, roll(low[v], -a), 0.0)
                dst[face(v, a, 0), :] = dst[face(v, a, 0), :] + x
                x = jnp.where(slot6 == EA - 1, roll(high[v], EA - 1 - a), 0.0)
                dst[face(v, a, N - 1), :] = dst[face(v, a, N - 1), :] + x

    def interface(section, digit, dst, scale):
        whole = lax.rem(frac_ref[section] // FRACS, EA)
        fraction = lax.rem(frac_ref[section], FRACS).astype(f32) / FRACS
        start = jnp.where(is_rotor, whole, EA - 1 - whole)
        scaled = by_sublane((POINTS + 1.0) / 2.0, N)
        rotor_up = jnp.where(scaled + fraction >= 1.0, 1.0, 0.0)
        stator_up = jnp.where(scaled > fraction, 1.0, 0.0)
        upper = jnp.where(is_rotor, rotor_up, stator_up)
        signed = jnp.where(is_rotor, scaled + fraction, scaled - fraction)
        base = jnp.where(is_rotor, 0.0, 1.0)
        local = (signed + base - upper) * 2.0 - 1.0
        weights = []
        for source in range(N):
            weight = jnp.ones_like(local)
            for another in range(N):
                if another != source:
                    weight = weight * (
                        (local - f32(POINTS[another]))
                        * f32(1.0 / (POINTS[source] - POINTS[another]))
                    )
            weights.append(weight)
        bits = [(start // s) % 2 == 1 for s in (1, 2, 4)]
        packed = []
        for t in range(8):
            held = [pair_in[section, h, pl.ds(N * t, N), :] for h in range(last_radix + 1)]
            first = choose(digit, held[1:])
            second = choose(digit, held[:-1])
            for bit, s in zip(bits, (1, 2, 4)):
                moved = jnp.where(slot6 < EA - s, roll(first, -s), roll(second, EA - s))
                first = jnp.where(bit, moved, first)
                second = jnp.where(bit, roll(second, -s), second)
            after = jnp.where(slot6 < EA - 1, roll(first, -1), roll(second, EA - 1))
            value = None
            for s in range(N):
                here = jnp.where(upper > 0.5, after[s : s + 1], first[s : s + 1])
                value = weights[s] * here if value is None else value + weights[s] * here
            packed.append(jnp.where(is_rotor, roll(value, LANES - SLAB), value))
        begin = jnp.where(is_rotor, LANES - SLAB, 0)
        valid = (lane6 >= begin) & (lane6 < begin + SLAB)
        sign = jnp.where(is_rotor, -1.0, 1.0)
        for b in range(N):
            outside = []
            for v in range(V):
                n = v * N + b
                outside.append(jnp.where(valid, roll(packed[n // 4], -SLAB * (n % 4)), 0.0))
            terms = jumps(outside, None, 3, sign, scale * LIFT, other_axial, other_sound)
            for v in range(V):
                rows = pl.ds(tile(v, own_a, b), N)
                dst[rows, :] = dst[rows, :] + terms[v]

    def run_section(section, src, dst, base, scale, ready=None):
        pack(src)
        if ready is not None:
            ready()
        first, halos = send_first(section)
        volume(src, dst, base, scale)
        last, digit = forward(section, first)
        inner_faces(src, dst, scale)
        for c in halos:
            c.wait()
        halo_faces(section, dst, scale)
        for c in last:
            c.wait()
        interface(section, digit, dst, scale)

    run_section(
        0,
        u_ref,
        w_ref,
        lambda v, a, b: get(u_ref, v, a, b),
        TIME_STEP,
        lambda: pl.semaphore_wait(barrier, len(targets)),
    )
    run_section(
        1,
        w_ref,
        u_ref,
        lambda v, a, b: 0.5 * (get(u_ref, v, a, b) + get(w_ref, v, a, b)),
        0.5 * TIME_STEP,
    )

    def store_state(a, carry):
        for v in range(V):
            for b in range(N):
                out_ref[v, a, b] = u_ref[pl.ds(tile(v, a, b), N), :]
        return carry

    lax.fori_loop(0, N, store_state, 0)


def solution(mesh):
    sectors = mesh.shape["sector"]
    stages = stages_of(sectors)
    n_sems = 2 + sum(radix for _, radix in stages) + len(stages)
    most = max(radix for _, radix in stages)

    def per_device(state, mean_flow, sector_offset, frac_index):
        table = jnp.asarray(DMAT, f32)
        smem = pl.BlockSpec(memory_space=pltpu.SMEM)
        vmem = pl.BlockSpec(memory_space=pltpu.VMEM)
        rows = V * N * N * 8
        return pl.pallas_call(
            functools.partial(kernel, sectors),
            out_shape=jax.ShapeDtypeStruct(state.shape, f32),
            in_specs=[smem, smem, smem, smem, vmem],
            out_specs=vmem,
            scratch_shapes=[
                pltpu.VMEM((rows, LANES), f32),
                pltpu.VMEM((rows, LANES), f32),
                pltpu.VMEM((V, 8, LANES), f32),
                pltpu.VMEM((V, 8, LANES), f32),
                pltpu.VMEM((2, V, 8, LANES), f32),
                pltpu.VMEM((2, V, 8, LANES), f32),
                pltpu.VMEM((TRACE_ROWS, LANES), f32),
                pltpu.VMEM((2, max(len(stages) - 1, 1), most, TRACE_ROWS, LANES), f32),
                pltpu.VMEM((2, stages[-1][1] + 1, TRACE_ROWS, LANES), f32),
                pltpu.SemaphoreType.DMA((2, n_sems)),
                pltpu.SemaphoreType.DMA((2, n_sems)),
            ],
            compiler_params=pltpu.CompilerParams(collective_id=0, has_side_effects=True),
        )(mean_flow, sector_offset, frac_index, table, state)

    spec = P(None, None, None, None, ("blk", "sector"))
    return jax.shard_map(
        per_device, mesh=mesh, in_specs=(spec, P(), P(), P()), out_specs=spec, check_vma=False
    )
```

```python
import functools
import math

import jax
import jax.numpy as jnp
import numpy as np
from jax import lax
from jax.experimental import pallas as pl
from jax.experimental.pallas import tpu as pltpu
from jax.sharding import PartitionSpec as P

FRACS = 4
EA = 8
ER = 4
EZ = 4
TIME_STEP = 0.02
V = 5
N = 6
LANES = 128
SLAB = EA * ER
TRACE_ROWS = 48
f32 = jnp.float32
MESH = pl.DeviceIdType.MESH


def lobatto_points():
    outer = math.sqrt(1.0 / 3.0 + 2.0 * math.sqrt(7.0) / 21.0)
    inner = math.sqrt(1.0 / 3.0 - 2.0 * math.sqrt(7.0) / 21.0)
    return np.array([-1.0, -outer, -inner, inner, outer, 1.0])


def derivative_matrix(points):
    number = points.shape[0]
    bary = np.array(
        [
            1.0 / np.prod([points[c] - points[o] for o in range(number) if o != c])
            for c in range(number)
        ]
    )
    matrix = np.zeros((number, number))
    for t in range(number):
        for s in range(number):
            if t != s:
                matrix[t, s] = bary[s] / bary[t] / (points[t] - points[s])
    return matrix


POINTS = lobatto_points()
DMAT = derivative_matrix(POINTS)
LIFT = N * (N - 1) / 2.0
HALF = 0.5 * LIFT


def split_cycle(count):
    group = math.gcd(count, 4)
    return group, count // group


def roll(x, by):
    by = by % LANES
    return x if by == 0 else pltpu.roll(x, by, 1)


def tile(v, a, b):
    return pl.multiple_of(((v * N + a) * N + b) * 8, 8)


def get(ref, v, a, b):
    return ref[pl.ds(tile(v, a, b), 8), :]


def choose(digit, options):
    out = options[0]
    for k in range(1, len(options)):
        out = jnp.where(digit == k, options[k], out)
    return out


def face(v, a, c):
    return pl.ds((v * N + a) * N * 8 + c, N, stride=8)


def by_sublane(values, rows):
    index = lax.broadcasted_iota(jnp.int32, (rows, LANES), 0)
    out = jnp.zeros((rows, LANES), f32)
    for k, value in enumerate(values):
        out = jnp.where(index == k, f32(value), out)
    return out


def kernel(
    sectors,
    flow_ref,
    offset_ref,
    frac_ref,
    dtab_ref,
    state_ref,
    out_ref,
    u_ref,
    w_ref,
    west_out,
    east_out,
    west_in,
    east_in,
    trace_out,
    hop_in,
    pair_out,
    pair_in,
    send_sem,
    recv_sem,
):
    group, groups = split_cycle(sectors)
    row = lax.axis_index("blk")
    me = lax.axis_index("sector")
    member = lax.rem(me, group)
    is_rotor = row == 0

    def around(off):
        return (row, lax.rem(me + off + sectors, sectors))

    def across(digit):
        return (1 - row, lax.rem(me + digit * group, sectors))

    def within(step):
        return (row, me - member + lax.rem(member + step, group))

    partners = [around(-1), around(1)]
    partners += [across(h) for h in range(groups)]
    partners += [within(g) for g in range(1, group)]
    barrier = pltpu.get_barrier_semaphore()
    for partner in partners:
        pl.semaphore_signal(barrier, inc=1, device_id=partner, device_id_type=MESH)

    lane = lax.broadcasted_iota(jnp.int32, (8, LANES), 1)
    lane6 = lane[:N]
    slot6 = lane6 % EA
    radial = (lane // EA) % ER
    s1 = 2.0 / (1.0 + (radial.astype(f32) + 0.5) / ER)
    s1_6 = s1[:N]

    def pick(k):
        return jnp.where(is_rotor, flow_ref[0, k], flow_ref[1, k])

    speed = [pick(k) for k in range(3)]
    sound = pick(3)
    other_axial = jnp.where(is_rotor, flow_ref[1, 2], flow_ref[0, 2])
    other_sound = jnp.where(is_rotor, flow_ref[1, 3], flow_ref[0, 3])
    top_sound = jnp.maximum(flow_ref[0, 3], flow_ref[1, 3])
    spread = [
        jnp.maximum(jnp.abs(flow_ref[0, k]), jnp.abs(flow_ref[1, k])) + top_sound for k in range(3)
    ]
    dcols = [by_sublane(DMAT[:, j], 8) for j in range(N)]
    own_a = jnp.where(is_rotor, N - 1, 0)

    def load_state(a, carry):
        for v in range(V):
            for b in range(N):
                u_ref[pl.ds(tile(v, a, b), N), :] = state_ref[v, a, b]
        return carry

    lax.fori_loop(0, N, load_state, 0)

    def pack_halo(ref):
        for v in range(V):
            left = jnp.zeros((N, LANES), f32)
            right = jnp.zeros((N, LANES), f32)
            for a in range(N):
                left = jnp.where(slot6 == a, roll(ref[face(v, a, 0), :], a), left)
                right = jnp.where(slot6 == a, roll(ref[face(v, a, N - 1), :], a - EA + 1), right)
            west_out[v, pl.ds(0, N), :] = left
            east_out[v, pl.ds(0, N), :] = right

    def pack_trace(ref):
        quarter = lane6 // SLAB
        turned = jnp.where(is_rotor, (quarter + 1) % 4, quarter)
        for t in range(8):
            merged = jnp.zeros((N, LANES), f32)
            for q in range(4):
                n = 4 * t + q
                if n < V * N:
                    here = ref[pl.ds(tile(n // N, own_a, n % N), N), :]
                    merged = jnp.where(turned == q, roll(here, SLAB * q), merged)
            trace_out[pl.ds(N * t, N), :] = jnp.where(is_rotor, roll(merged, SLAB), merged)

    def copy(section, k, src, dst, target):
        return pltpu.make_async_remote_copy(
            src_ref=src,
            dst_ref=dst,
            send_sem=send_sem.at[section, k],
            recv_sem=recv_sem.at[section, k],
            device_id=target,
            device_id_type=MESH,
        )

    def send_across(section):
        copies = [
            copy(section, 2 + h, trace_out, hop_in.at[section, h], across(h))
            for h in reversed(range(groups))
        ]
        for c in copies:
            c.start()
        return copies

    def send_halos(section):
        copies = [
            copy(section, 0, west_out, west_in.at[section], around(-1)),
            copy(section, 1, east_out, east_in.at[section], around(1)),
        ]
        for c in copies:
            c.start()
        return copies

    def send_within(section):
        amount = jnp.where(
            is_rotor,
            lax.rem(2 * sectors - offset_ref[section] - 1, sectors),
            lax.rem(offset_ref[section], sectors),
        )
        high, low = amount // group, lax.rem(amount, group)
        arrived = [hop_in[section, h] for h in range(groups)]
        facing = choose(lax.rem(high + (member + low) // group, groups), arrived)
        prior = choose(lax.rem(high + (member + low + 1) // group, groups), arrived)
        copies = []
        for g in range(1, group):
            pair_out[g - 1] = jnp.where(low == g, facing, prior)
            copies.append(
                copy(
                    section,
                    1 + groups + g,
                    pair_out.at[g - 1],
                    pair_in.at[section, g],
                    within(g),
                )
            )
            copies[-1].start()
        pair_in[section, 0] = jnp.where(low == 0, facing, prior)
        return copies, low

    def volume(src, dst, base, scale):
        k1 = -scale * s1 * speed[0]
        c1 = -scale * s1 * sound
        k2 = jnp.full((8, LANES), -2.0 * scale * speed[1], f32)
        k3 = jnp.full((8, LANES), -2.0 * scale * speed[2], f32)
        c2 = jnp.full((8, LANES), -2.0 * scale * sound, f32)

        def at_b(b, carry):
            row_b = [dtab_ref[b, j] for j in range(N)]
            for a in range(N):
                kept = {}
                zero_sum = None
                for v in range(V):
                    start = tile(v, a, b)
                    g1 = dcols[0] * src[pl.ds(start, 1), :]
                    for j in range(1, N):
                        g1 = g1 + dcols[j] * src[pl.ds(start + j, 1), :]
                    g2 = row_b[0] * get(src, v, a, 0)
                    for j in range(1, N):
                        g2 = g2 + row_b[j] * get(src, v, a, j)
                    g3 = None
                    for j in range(N):
                        if j != a:
                            term = f32(DMAT[a, j]) * get(src, v, j, b)
                            g3 = term if g3 is None else g3 + term
                    total = base(v, a, b) + k1 * g1 + k2 * g2 + k3 * g3
                    if v == 0:
                        kept = {1: g1, 2: g2, 3: g3}
                        zero_sum = total
                        continue
                    if v == 1:
                        total = total + c1 * kept[1]
                        zero_sum = zero_sum + c1 * g1
                    if v == 2:
                        total = total + c2 * kept[2]
                        zero_sum = zero_sum + c2 * g2
                    if v == 3:
                        total = total + c2 * kept[3]
                        zero_sum = zero_sum + c2 * g3
                    dst[pl.ds(start, 8), :] = total
                dst[pl.ds(tile(0, a, b), 8), :] = zero_sum
            return carry

        lax.fori_loop(0, N, at_b, 0)

    def jumps(outside, inside, direction, sign, factor, along, acoustic):
        result = []
        for v in range(V):
            flux = along * outside[v]
            if v == 0:
                flux = flux + acoustic * outside[direction]
            if v == direction:
                flux = flux + acoustic * outside[0]
            gap = outside[v] if inside is None else outside[v] - inside[v]
            result.append(factor * (sign * flux + spread[direction - 1] * gap))
        return result

    def inner_faces(src, dst, scale):
        def azimuthal(a, carry):
            lows = [src[face(v, a, 0), :] for v in range(V)]
            highs = [src[face(v, a, N - 1), :] for v in range(V)]
            before = [jnp.where(slot6 == 0, 0.0, roll(x, 1)) for x in highs]
            after = [jnp.where(slot6 == EA - 1, 0.0, roll(x, -1)) for x in lows]
            factor = scale * HALF * s1_6
            for c, out, ins, sign in ((0, before, lows, 1.0), (N - 1, after, highs, -1.0)):
                for v, x in enumerate(jumps(out, ins, 1, sign, factor, speed[0], sound)):
                    dst[face(v, a, c), :] = dst[face(v, a, c), :] + x
            return carry

        lax.fori_loop(0, N, azimuthal, 0)

        def radial_faces(a, carry):
            lows = [get(src, v, a, 0) for v in range(V)]
            highs = [get(src, v, a, N - 1) for v in range(V)]
            below = [
                jnp.where(radial == 0, -lows[v] if v == 2 else lows[v], roll(highs[v], EA))
                for v in range(V)
            ]
            above = [
                jnp.where(radial == ER - 1, -highs[v] if v == 2 else highs[v], roll(lows[v], -EA))
                for v in range(V)
            ]
            factor = scale * LIFT
            for b, out, ins, sign in ((0, below, lows, 1.0), (N - 1, above, highs, -1.0)):
                for v, x in enumerate(jumps(out, ins, 2, sign, factor, speed[1], sound)):
                    dst[pl.ds(tile(v, a, b), 8), :] = get(dst, v, a, b) + x
            return carry

        lax.fori_loop(0, N, radial_faces, 0)

        def axial_faces(b, carry):
            lows = [get(src, v, 0, b) for v in range(V)]
            highs = [get(src, v, N - 1, b) for v in range(V)]
            below = [jnp.where(lane < SLAB, 0.0, roll(x, SLAB)) for x in highs]
            above = [jnp.where(lane >= LANES - SLAB, 0.0, roll(x, -SLAB)) for x in lows]
            factor = scale * LIFT
            for a, out, ins, sign in ((0, below, lows, 1.0), (N - 1, above, highs, -1.0)):
                for v, x in enumerate(jumps(out, ins, 3, sign, factor, speed[2], sound)):
                    dst[pl.ds(tile(v, a, b), 8), :] = get(dst, v, a, b) + x
            return carry

        lax.fori_loop(0, N, axial_faces, 0)

    def halo_faces(section, dst, scale):
        factor = scale * HALF * s1_6
        from_west = [east_in[section, v, pl.ds(0, N), :] for v in range(V)]
        from_east = [west_in[section, v, pl.ds(0, N), :] for v in range(V)]
        low = jumps(from_west, None, 1, 1.0, factor, speed[0], sound)
        high = jumps(from_east, None, 1, -1.0, factor, speed[0], sound)
        for v in range(V):
            for a in range(N):
                x = jnp.where(slot6 == 0, roll(low[v], -a), 0.0)
                dst[face(v, a, 0), :] = dst[face(v, a, 0), :] + x
                x = jnp.where(slot6 == EA - 1, roll(high[v], EA - 1 - a), 0.0)
                dst[face(v, a, N - 1), :] = dst[face(v, a, N - 1), :] + x

    def interface(section, digit, dst, scale):
        whole = lax.rem(frac_ref[section] // FRACS, EA)
        fraction = lax.rem(frac_ref[section], FRACS).astype(f32) / FRACS
        start = jnp.where(is_rotor, whole, EA - 1 - whole)
        scaled = by_sublane((POINTS + 1.0) / 2.0, N)
        rotor_up = jnp.where(scaled + fraction >= 1.0, 1.0, 0.0)
        stator_up = jnp.where(scaled > fraction, 1.0, 0.0)
        upper = jnp.where(is_rotor, rotor_up, stator_up)
        signed = jnp.where(is_rotor, scaled + fraction, scaled - fraction)
        base = jnp.where(is_rotor, 0.0, 1.0)
        local = (signed + base - upper) * 2.0 - 1.0
        weights = []
        for source in range(N):
            weight = jnp.ones_like(local)
            for another in range(N):
                if another != source:
                    weight = weight * (
                        (local - f32(POINTS[another]))
                        * f32(1.0 / (POINTS[source] - POINTS[another]))
                    )
            weights.append(weight)
        bits = [(start // s) % 2 == 1 for s in (1, 2, 4)]
        packed = []
        for t in range(8):
            held = [pair_in[section, g, pl.ds(N * t, N), :] for g in range(group)]
            first = choose(digit, held[1:] + held[:1])
            second = choose(digit, held)
            for bit, s in zip(bits, (1, 2, 4)):
                moved = jnp.where(slot6 < EA - s, roll(first, -s), roll(second, EA - s))
                first = jnp.where(bit, moved, first)
                second = jnp.where(bit, roll(second, -s), second)
            after = jnp.where(slot6 < EA - 1, roll(first, -1), roll(second, EA - 1))
            value = None
            for s in range(N):
                here = jnp.where(upper > 0.5, after[s : s + 1], first[s : s + 1])
                value = weights[s] * here if value is None else value + weights[s] * here
            packed.append(jnp.where(is_rotor, roll(value, LANES - SLAB), value))
        begin = jnp.where(is_rotor, LANES - SLAB, 0)
        valid = (lane6 >= begin) & (lane6 < begin + SLAB)
        sign = jnp.where(is_rotor, -1.0, 1.0)
        for b in range(N):
            outside = []
            for v in range(V):
                n = v * N + b
                outside.append(jnp.where(valid, roll(packed[n // 4], -SLAB * (n % 4)), 0.0))
            terms = jumps(outside, None, 3, sign, scale * LIFT, other_axial, other_sound)
            for v in range(V):
                rows = pl.ds(tile(v, own_a, b), N)
                dst[rows, :] = dst[rows, :] + terms[v]

    def run_section(section, src, dst, base, scale, ready=None):
        pack_trace(src)
        if ready is not None:
            ready()
        first = send_across(section)
        pack_halo(src)
        halos = send_halos(section)
        volume(src, dst, base, scale)
        inner_faces(src, dst, scale)
        for c in first:
            c.wait()
        last, digit = send_within(section)
        for c in halos:
            c.wait()
        halo_faces(section, dst, scale)
        for c in last:
            c.wait()
        interface(section, digit, dst, scale)

    run_section(
        0,
        u_ref,
        w_ref,
        lambda v, a, b: get(u_ref, v, a, b),
        TIME_STEP,
        lambda: pl.semaphore_wait(barrier, len(partners)),
    )
    run_section(
        1,
        w_ref,
        u_ref,
        lambda v, a, b: 0.5 * (get(u_ref, v, a, b) + get(w_ref, v, a, b)),
        0.5 * TIME_STEP,
    )

    def store_state(a, carry):
        for v in range(V):
            for b in range(N):
                out_ref[v, a, b] = u_ref[pl.ds(tile(v, a, b), N), :]
        return carry

    lax.fori_loop(0, N, store_state, 0)


def solution(mesh):
    sectors = mesh.shape["sector"]
    group, groups = split_cycle(sectors)
    n_sems = 1 + groups + group

    def per_device(state, mean_flow, sector_offset, frac_index):
        table = jnp.asarray(DMAT, f32)
        smem = pl.BlockSpec(memory_space=pltpu.SMEM)
        vmem = pl.BlockSpec(memory_space=pltpu.VMEM)
        rows = V * N * N * 8
        return pl.pallas_call(
            functools.partial(kernel, sectors),
            out_shape=jax.ShapeDtypeStruct(state.shape, f32),
            in_specs=[smem, smem, smem, smem, vmem],
            out_specs=vmem,
            scratch_shapes=[
                pltpu.VMEM((rows, LANES), f32),
                pltpu.VMEM((rows, LANES), f32),
                pltpu.VMEM((V, 8, LANES), f32),
                pltpu.VMEM((V, 8, LANES), f32),
                pltpu.VMEM((2, V, 8, LANES), f32),
                pltpu.VMEM((2, V, 8, LANES), f32),
                pltpu.VMEM((TRACE_ROWS, LANES), f32),
                pltpu.VMEM((2, groups, TRACE_ROWS, LANES), f32),
                pltpu.VMEM((max(group - 1, 1), TRACE_ROWS, LANES), f32),
                pltpu.VMEM((2, group, TRACE_ROWS, LANES), f32),
                pltpu.SemaphoreType.DMA((2, n_sems)),
                pltpu.SemaphoreType.DMA((2, n_sems)),
            ],
            compiler_params=pltpu.CompilerParams(collective_id=0, has_side_effects=True),
        )(mean_flow, sector_offset, frac_index, table, state)

    spec = P(None, None, None, None, ("blk", "sector"))
    return jax.shard_map(
        per_device, mesh=mesh, in_specs=(spec, P(), P(), P()), out_specs=spec, check_vma=False
    )
```

```python
import functools
import math

import jax
import jax.numpy as jnp
import numpy as np
from jax import lax
from jax.experimental import pallas as pl
from jax.experimental.pallas import tpu as pltpu
from jax.sharding import PartitionSpec as P

FRACS = 4
EA = 8
ER = 4
EZ = 4
TIME_STEP = 0.02
V = 5
N = 6
LANES = 128
SLAB = EA * ER
TRACE_ROWS = 48
f32 = jnp.float32
MESH = pl.DeviceIdType.MESH


def lobatto_points():
    outer = math.sqrt(1.0 / 3.0 + 2.0 * math.sqrt(7.0) / 21.0)
    inner = math.sqrt(1.0 / 3.0 - 2.0 * math.sqrt(7.0) / 21.0)
    return np.array([-1.0, -outer, -inner, inner, outer, 1.0])


def derivative_matrix(points):
    number = points.shape[0]
    bary = np.array(
        [
            1.0 / np.prod([points[c] - points[o] for o in range(number) if o != c])
            for c in range(number)
        ]
    )
    matrix = np.zeros((number, number))
    for t in range(number):
        for s in range(number):
            if t != s:
                matrix[t, s] = bary[s] / bary[t] / (points[t] - points[s])
    return matrix


POINTS = lobatto_points()
DMAT = derivative_matrix(POINTS)
LIFT = N * (N - 1) / 2.0
HALF = 0.5 * LIFT


def split_cycle(count):
    group = math.gcd(count, 4)
    return group, count // group


def roll(x, by):
    by = by % LANES
    return x if by == 0 else pltpu.roll(x, by, 1)


def tile(v, a, b):
    return pl.multiple_of(((v * N + a) * N + b) * 8, 8)


def get(ref, v, a, b):
    return ref[pl.ds(tile(v, a, b), 8), :]


def choose(digit, options):
    out = options[0]
    for k in range(1, len(options)):
        out = jnp.where(digit == k, options[k], out)
    return out


def face(v, a, c):
    return pl.ds((v * N + a) * N * 8 + c, N, stride=8)


def by_sublane(values, rows):
    index = lax.broadcasted_iota(jnp.int32, (rows, LANES), 0)
    out = jnp.zeros((rows, LANES), f32)
    for k, value in enumerate(values):
        out = jnp.where(index == k, f32(value), out)
    return out


def kernel(
    sectors,
    flow_hbm,
    offset_hbm,
    frac_hbm,
    state_hbm,
    out_ref,
    flow_ref,
    offset_ref,
    frac_ref,
    state_ref,
    face_ref,
    u_ref,
    w_ref,
    west_out,
    east_out,
    west_in,
    east_in,
    trace_out,
    hop_in,
    pair_out,
    pair_in,
    load_sem,
    send_sem,
    recv_sem,
):
    group, groups = split_cycle(sectors)
    row = lax.axis_index("blk")
    me = lax.axis_index("sector")
    member = lax.rem(me, group)
    is_rotor = row == 0

    def around(off):
        return (row, lax.rem(me + off + sectors, sectors))

    def across(digit):
        return (1 - row, lax.rem(me + digit * group, sectors))

    def within(step):
        return (row, me - member + lax.rem(member + step, group))

    partners = [around(-1), around(1)]
    partners += [across(h) for h in range(groups)]
    partners += [within(g) for g in range(1, group)]
    barrier = pltpu.get_barrier_semaphore()
    for partner in partners:
        pl.semaphore_signal(barrier, inc=1, device_id=partner, device_id_type=MESH)

    own_a = jnp.where(is_rotor, N - 1, 0)
    loads = [
        pltpu.make_async_copy(src, dst, load_sem.at[k])
        for k, (src, dst) in enumerate(
            (
                (state_hbm.at[:, own_a], face_ref),
                (flow_hbm, flow_ref),
                (offset_hbm, offset_ref),
                (frac_hbm, frac_ref),
                (state_hbm, state_ref),
            )
        )
    ]
    for c in loads:
        c.start()

    lane = lax.broadcasted_iota(jnp.int32, (8, LANES), 1)
    lane6 = lane[:N]
    slot6 = lane6 % EA
    radial = (lane // EA) % ER
    s1 = 2.0 / (1.0 + (radial.astype(f32) + 0.5) / ER)
    s1_6 = s1[:N]

    for c in loads[1:4]:
        c.wait()

    def pick(k):
        return jnp.where(is_rotor, flow_ref[0, k], flow_ref[1, k])

    speed = [pick(k) for k in range(3)]
    sound = pick(3)
    other_axial = jnp.where(is_rotor, flow_ref[1, 2], flow_ref[0, 2])
    other_sound = jnp.where(is_rotor, flow_ref[1, 3], flow_ref[0, 3])
    top_sound = jnp.maximum(flow_ref[0, 3], flow_ref[1, 3])
    spread = [
        jnp.maximum(jnp.abs(flow_ref[0, k]), jnp.abs(flow_ref[1, k])) + top_sound for k in range(3)
    ]
    dcols = [by_sublane(DMAT[:, j], 8) for j in range(N)]
    def load_state(a, carry):
        for v in range(V):
            for b in range(N):
                u_ref[pl.ds(tile(v, a, b), N), :] = state_ref[v, a, b]
        return carry

    def pack_halo(ref):
        for v in range(V):
            left = jnp.zeros((N, LANES), f32)
            right = jnp.zeros((N, LANES), f32)
            for a in range(N):
                left = jnp.where(slot6 == a, roll(ref[face(v, a, 0), :], a), left)
                right = jnp.where(slot6 == a, roll(ref[face(v, a, N - 1), :], a - EA + 1), right)
            west_out[v, pl.ds(0, N), :] = left
            east_out[v, pl.ds(0, N), :] = right

    def pack_trace(read):
        quarter = lane6 // SLAB
        turned = jnp.where(is_rotor, (quarter + 1) % 4, quarter)
        for t in range(8):
            merged = jnp.zeros((N, LANES), f32)
            for q in range(4):
                n = 4 * t + q
                if n < V * N:
                    here = read(n // N, n % N)
                    merged = jnp.where(turned == q, roll(here, SLAB * q), merged)
            trace_out[pl.ds(N * t, N), :] = jnp.where(is_rotor, roll(merged, SLAB), merged)

    def copy(section, k, src, dst, target):
        return pltpu.make_async_remote_copy(
            src_ref=src,
            dst_ref=dst,
            send_sem=send_sem.at[section, k],
            recv_sem=recv_sem.at[section, k],
            device_id=target,
            device_id_type=MESH,
        )

    def send_across(section):
        copies = [
            copy(section, 2 + h, trace_out, hop_in.at[section, h], across(h))
            for h in sorted(range(groups), key=lambda h: -min(h, groups - h))
        ]
        for c in copies:
            c.start()
        return copies

    def send_halos(section):
        copies = [
            copy(section, 0, west_out, west_in.at[section], around(-1)),
            copy(section, 1, east_out, east_in.at[section], around(1)),
        ]
        for c in copies:
            c.start()
        return copies

    def send_within(section):
        amount = jnp.where(
            is_rotor,
            lax.rem(2 * sectors - offset_ref[section] - 1, sectors),
            lax.rem(offset_ref[section], sectors),
        )
        high, low = amount // group, lax.rem(amount, group)
        arrived = [hop_in[section, h] for h in range(groups)]
        facing = choose(lax.rem(high + (member + low) // group, groups), arrived)
        prior = choose(lax.rem(high + (member + low + 1) // group, groups), arrived)
        copies = []
        for g in range(1, group):
            pair_out[g - 1] = jnp.where(low == g, facing, prior)
            copies.append(
                copy(
                    section,
                    1 + groups + g,
                    pair_out.at[g - 1],
                    pair_in.at[section, g],
                    within(g),
                )
            )
            copies[-1].start()
        pair_in[section, 0] = jnp.where(low == 0, facing, prior)
        return copies, low

    def volume(src, dst, base, scale):
        k1 = -scale * s1 * speed[0]
        c1 = -scale * s1 * sound
        k2 = jnp.full((8, LANES), -2.0 * scale * speed[1], f32)
        k3 = jnp.full((8, LANES), -2.0 * scale * speed[2], f32)
        c2 = jnp.full((8, LANES), -2.0 * scale * sound, f32)

        def at_b(b, carry):
            row_b = [choose(b, [f32(DMAT[k, j]) for k in range(N)]) for j in range(N)]
            for a in range(N):
                kept = {}
                zero_sum = None
                for v in range(V):
                    start = tile(v, a, b)
                    g1 = dcols[0] * src[pl.ds(start, 1), :]
                    for j in range(1, N):
                        g1 = g1 + dcols[j] * src[pl.ds(start + j, 1), :]
                    g2 = row_b[0] * get(src, v, a, 0)
                    for j in range(1, N):
                        g2 = g2 + row_b[j] * get(src, v, a, j)
                    g3 = None
                    for j in range(N):
                        if j != a:
                            term = f32(DMAT[a, j]) * get(src, v, j, b)
                            g3 = term if g3 is None else g3 + term
                    total = base(v, a, b) + k1 * g1 + k2 * g2 + k3 * g3
                    if v == 0:
                        kept = {1: g1, 2: g2, 3: g3}
                        zero_sum = total
                        continue
                    if v == 1:
                        total = total + c1 * kept[1]
                        zero_sum = zero_sum + c1 * g1
                    if v == 2:
                        total = total + c2 * kept[2]
                        zero_sum = zero_sum + c2 * g2
                    if v == 3:
                        total = total + c2 * kept[3]
                        zero_sum = zero_sum + c2 * g3
                    dst[pl.ds(start, 8), :] = total
                dst[pl.ds(tile(0, a, b), 8), :] = zero_sum
            return carry

        lax.fori_loop(0, N, at_b, 0)

    def jumps(outside, inside, direction, sign, factor, along, acoustic):
        result = []
        for v in range(V):
            flux = along * outside[v]
            if v == 0:
                flux = flux + acoustic * outside[direction]
            if v == direction:
                flux = flux + acoustic * outside[0]
            gap = outside[v] if inside is None else outside[v] - inside[v]
            result.append(factor * (sign * flux + spread[direction - 1] * gap))
        return result

    def inner_faces(src, dst, scale):
        def azimuthal(a, carry):
            lows = [src[face(v, a, 0), :] for v in range(V)]
            highs = [src[face(v, a, N - 1), :] for v in range(V)]
            before = [jnp.where(slot6 == 0, 0.0, roll(x, 1)) for x in highs]
            after = [jnp.where(slot6 == EA - 1, 0.0, roll(x, -1)) for x in lows]
            factor = scale * HALF * s1_6
            for c, out, ins, sign in ((0, before, lows, 1.0), (N - 1, after, highs, -1.0)):
                for v, x in enumerate(jumps(out, ins, 1, sign, factor, speed[0], sound)):
                    dst[face(v, a, c), :] = dst[face(v, a, c), :] + x
            return carry

        lax.fori_loop(0, N, azimuthal, 0)

        def radial_faces(a, carry):
            lows = [get(src, v, a, 0) for v in range(V)]
            highs = [get(src, v, a, N - 1) for v in range(V)]
            below = [
                jnp.where(radial == 0, -lows[v] if v == 2 else lows[v], roll(highs[v], EA))
                for v in range(V)
            ]
            above = [
                jnp.where(radial == ER - 1, -highs[v] if v == 2 else highs[v], roll(lows[v], -EA))
                for v in range(V)
            ]
            factor = scale * LIFT
            for b, out, ins, sign in ((0, below, lows, 1.0), (N - 1, above, highs, -1.0)):
                for v, x in enumerate(jumps(out, ins, 2, sign, factor, speed[1], sound)):
                    dst[pl.ds(tile(v, a, b), 8), :] = get(dst, v, a, b) + x
            return carry

        lax.fori_loop(0, N, radial_faces, 0)

        def axial_faces(b, carry):
            lows = [get(src, v, 0, b) for v in range(V)]
            highs = [get(src, v, N - 1, b) for v in range(V)]
            below = [jnp.where(lane < SLAB, 0.0, roll(x, SLAB)) for x in highs]
            above = [jnp.where(lane >= LANES - SLAB, 0.0, roll(x, -SLAB)) for x in lows]
            factor = scale * LIFT
            for a, out, ins, sign in ((0, below, lows, 1.0), (N - 1, above, highs, -1.0)):
                for v, x in enumerate(jumps(out, ins, 3, sign, factor, speed[2], sound)):
                    dst[pl.ds(tile(v, a, b), 8), :] = get(dst, v, a, b) + x
            return carry

        lax.fori_loop(0, N, axial_faces, 0)

    def halo_faces(section, dst, scale):
        factor = scale * HALF * s1_6
        from_west = [east_in[section, v, pl.ds(0, N), :] for v in range(V)]
        from_east = [west_in[section, v, pl.ds(0, N), :] for v in range(V)]
        low = jumps(from_west, None, 1, 1.0, factor, speed[0], sound)
        high = jumps(from_east, None, 1, -1.0, factor, speed[0], sound)
        for v in range(V):
            for a in range(N):
                x = jnp.where(slot6 == 0, roll(low[v], -a), 0.0)
                dst[face(v, a, 0), :] = dst[face(v, a, 0), :] + x
                x = jnp.where(slot6 == EA - 1, roll(high[v], EA - 1 - a), 0.0)
                dst[face(v, a, N - 1), :] = dst[face(v, a, N - 1), :] + x

    def interface(section, digit, dst, scale):
        whole = lax.rem(frac_ref[section] // FRACS, EA)
        fraction = lax.rem(frac_ref[section], FRACS).astype(f32) / FRACS
        start = jnp.where(is_rotor, whole, EA - 1 - whole)
        scaled = by_sublane((POINTS + 1.0) / 2.0, N)
        rotor_up = jnp.where(scaled + fraction >= 1.0, 1.0, 0.0)
        stator_up = jnp.where(scaled > fraction, 1.0, 0.0)
        upper = jnp.where(is_rotor, rotor_up, stator_up)
        signed = jnp.where(is_rotor, scaled + fraction, scaled - fraction)
        base = jnp.where(is_rotor, 0.0, 1.0)
        local = (signed + base - upper) * 2.0 - 1.0
        weights = []
        for source in range(N):
            weight = jnp.ones_like(local)
            for another in range(N):
                if another != source:
                    weight = weight * (
                        (local - f32(POINTS[another]))
                        * f32(1.0 / (POINTS[source] - POINTS[another]))
                    )
            weights.append(weight)
        bits = [(start // s) % 2 == 1 for s in (1, 2, 4)]
        packed = []
        for t in range(8):
            held = [pair_in[section, g, pl.ds(N * t, N), :] for g in range(group)]
            first = choose(digit, held[1:] + held[:1])
            second = choose(digit, held)
            for bit, s in zip(bits, (1, 2, 4)):
                moved = jnp.where(slot6 < EA - s, roll(first, -s), roll(second, EA - s))
                first = jnp.where(bit, moved, first)
                second = jnp.where(bit, roll(second, -s), second)
            after = jnp.where(slot6 < EA - 1, roll(first, -1), roll(second, EA - 1))
            value = None
            for s in range(N):
                here = jnp.where(upper > 0.5, after[s : s + 1], first[s : s + 1])
                value = weights[s] * here if value is None else value + weights[s] * here
            packed.append(jnp.where(is_rotor, roll(value, LANES - SLAB), value))
        begin = jnp.where(is_rotor, LANES - SLAB, 0)
        valid = (lane6 >= begin) & (lane6 < begin + SLAB)
        sign = jnp.where(is_rotor, -1.0, 1.0)
        for b in range(N):
            outside = []
            for v in range(V):
                n = v * N + b
                outside.append(jnp.where(valid, roll(packed[n // 4], -SLAB * (n % 4)), 0.0))
            terms = jumps(outside, None, 3, sign, scale * LIFT, other_axial, other_sound)
            for v in range(V):
                rows = pl.ds(tile(v, own_a, b), N)
                dst[rows, :] = dst[rows, :] + terms[v]

    def run_section(section, first, src, dst, base, scale):
        pack_halo(src)
        halos = send_halos(section)
        volume(src, dst, base, scale)
        inner_faces(src, dst, scale)
        for c in first:
            c.wait()
        last, digit = send_within(section)
        for c in halos:
            c.wait()
        halo_faces(section, dst, scale)
        for c in last:
            c.wait()
        interface(section, digit, dst, scale)

    loads[0].wait()
    pack_trace(lambda v, b: face_ref[v, b])
    pl.semaphore_wait(barrier, len(partners))
    first = send_across(0)
    loads[4].wait()
    lax.fori_loop(0, N, load_state, 0)
    run_section(0, first, u_ref, w_ref, lambda v, a, b: get(u_ref, v, a, b), TIME_STEP)
    pack_trace(lambda v, b: w_ref[pl.ds(tile(v, own_a, b), N), :])
    run_section(
        1,
        send_across(1),
        w_ref,
        u_ref,
        lambda v, a, b: 0.5 * (get(u_ref, v, a, b) + get(w_ref, v, a, b)),
        0.5 * TIME_STEP,
    )

    def store_state(a, carry):
        for v in range(V):
            for b in range(N):
                out_ref[v, a, b] = u_ref[pl.ds(tile(v, a, b), N), :]
        return carry

    lax.fori_loop(0, N, store_state, 0)


def solution(mesh):
    sectors = mesh.shape["sector"]
    group, groups = split_cycle(sectors)
    n_sems = 1 + groups + group

    def per_device(state, mean_flow, sector_offset, frac_index):
        hbm = pl.BlockSpec(memory_space=pltpu.HBM)
        vmem = pl.BlockSpec(memory_space=pltpu.VMEM)
        rows = V * N * N * 8
        return pl.pallas_call(
            functools.partial(kernel, sectors),
            out_shape=pltpu.VMEM(state.shape, f32),
            in_specs=[hbm, hbm, hbm, hbm],
            out_specs=vmem,
            scratch_shapes=[
                pltpu.SMEM(mean_flow.shape, f32),
                pltpu.SMEM(sector_offset.shape, jnp.int32),
                pltpu.SMEM(frac_index.shape, jnp.int32),
                pltpu.VMEM(state.shape, f32),
                pltpu.VMEM((V, N, N, LANES), f32),
                pltpu.VMEM((rows, LANES), f32),
                pltpu.VMEM((rows, LANES), f32),
                pltpu.VMEM((V, 8, LANES), f32),
                pltpu.VMEM((V, 8, LANES), f32),
                pltpu.VMEM((2, V, 8, LANES), f32),
                pltpu.VMEM((2, V, 8, LANES), f32),
                pltpu.VMEM((TRACE_ROWS, LANES), f32),
                pltpu.VMEM((2, groups, TRACE_ROWS, LANES), f32),
                pltpu.VMEM((max(group - 1, 1), TRACE_ROWS, LANES), f32),
                pltpu.VMEM((2, group, TRACE_ROWS, LANES), f32),
                pltpu.SemaphoreType.DMA((5,)),
                pltpu.SemaphoreType.DMA((2, n_sems)),
                pltpu.SemaphoreType.DMA((2, n_sems)),
            ],
            compiler_params=pltpu.CompilerParams(collective_id=0, has_side_effects=True),
        )(mean_flow, sector_offset, frac_index, state)

    spec = P(None, None, None, None, ("blk", "sector"))
    return jax.shard_map(
        per_device, mesh=mesh, in_specs=(spec, P(), P(), P()), out_specs=spec, check_vma=False
    )
```

```python
import functools
import math

import jax
import jax.numpy as jnp
import numpy as np
from jax import lax
from jax.experimental import pallas as pl
from jax.experimental.pallas import tpu as pltpu
from jax.sharding import PartitionSpec as P

FRACS = 4
EA = 8
ER = 4
EZ = 4
TIME_STEP = 0.02
V = 5
N = 6
LANES = 128
SLAB = EA * ER
TRACE_ROWS = 48
f32 = jnp.float32
MESH = pl.DeviceIdType.MESH


def lobatto_points():
    outer = math.sqrt(1.0 / 3.0 + 2.0 * math.sqrt(7.0) / 21.0)
    inner = math.sqrt(1.0 / 3.0 - 2.0 * math.sqrt(7.0) / 21.0)
    return np.array([-1.0, -outer, -inner, inner, outer, 1.0])


def derivative_matrix(points):
    number = points.shape[0]
    bary = np.array(
        [
            1.0 / np.prod([points[c] - points[o] for o in range(number) if o != c])
            for c in range(number)
        ]
    )
    matrix = np.zeros((number, number))
    for t in range(number):
        for s in range(number):
            if t != s:
                matrix[t, s] = bary[s] / bary[t] / (points[t] - points[s])
    return matrix


POINTS = lobatto_points()
DMAT = derivative_matrix(POINTS)
LIFT = N * (N - 1) / 2.0
HALF = 0.5 * LIFT


def split_cycle(count):
    group = math.gcd(count, 4)
    return group, count // group


def roll(x, by):
    by = by % LANES
    return x if by == 0 else pltpu.roll(x, by, 1)


def turn(x, by):
    return pltpu.roll(x, lax.rem(by + 2 * LANES, LANES), 1)


def tile(v, a, b):
    return pl.multiple_of(((v * N + a) * N + b) * 8, 8)


def get(ref, v, a, b):
    return ref[pl.ds(tile(v, a, b), 8), :]


def choose(digit, options):
    out = options[0]
    for k in range(1, len(options)):
        out = jnp.where(digit == k, options[k], out)
    return out


def face(v, a, c):
    return pl.ds((v * N + a) * N * 8 + c, N, stride=8)


def by_sublane(values, rows):
    index = lax.broadcasted_iota(jnp.int32, (rows, LANES), 0)
    out = jnp.zeros((rows, LANES), f32)
    for k, value in enumerate(values):
        out = jnp.where(index == k, f32(value), out)
    return out


def kernel(
    sectors,
    flow_hbm,
    offset_hbm,
    frac_hbm,
    state_hbm,
    out_ref,
    flow_ref,
    offset_ref,
    frac_ref,
    state_ref,
    face_ref,
    u_ref,
    w_ref,
    west_out,
    east_out,
    west_in,
    east_in,
    trace_out,
    hop_in,
    pair_out,
    pair_in,
    load_sem,
    send_sem,
    recv_sem,
):
    group, groups = split_cycle(sectors)
    row = lax.axis_index("blk")
    me = lax.axis_index("sector")
    member = lax.rem(me, group)
    is_rotor = row == 0

    def around(off):
        return (row, lax.rem(me + off + sectors, sectors))

    def across(digit):
        return (1 - row, lax.rem(me + digit * group, sectors))

    def within(step):
        return (row, me - member + lax.rem(member + step, group))

    partners = [around(-1), around(1)]
    partners += [across(h) for h in range(groups)]
    partners += [within(g) for g in range(1, group)]
    barrier = pltpu.get_barrier_semaphore()
    for partner in partners:
        pl.semaphore_signal(barrier, inc=1, device_id=partner, device_id_type=MESH)

    own_a = jnp.where(is_rotor, N - 1, 0)
    loads = [
        pltpu.make_async_copy(src, dst, load_sem.at[k])
        for k, (src, dst) in enumerate(
            (
                (state_hbm.at[:, own_a], face_ref),
                (flow_hbm, flow_ref),
                (offset_hbm, offset_ref),
                (frac_hbm, frac_ref),
                (state_hbm, state_ref),
            )
        )
    ]
    for c in loads:
        c.start()

    lane = lax.broadcasted_iota(jnp.int32, (8, LANES), 1)
    lane6 = lane[:N]
    slot6 = lane6 % EA
    radial = (lane // EA) % ER
    s1 = 2.0 / (1.0 + (radial.astype(f32) + 0.5) / ER)
    s1_6 = s1[:N]

    for c in loads[1:4]:
        c.wait()

    def pick(k):
        return jnp.where(is_rotor, flow_ref[0, k], flow_ref[1, k])

    speed = [pick(k) for k in range(3)]
    sound = pick(3)
    other_axial = jnp.where(is_rotor, flow_ref[1, 2], flow_ref[0, 2])
    other_sound = jnp.where(is_rotor, flow_ref[1, 3], flow_ref[0, 3])
    top_sound = jnp.maximum(flow_ref[0, 3], flow_ref[1, 3])
    spread = [
        jnp.maximum(jnp.abs(flow_ref[0, k]), jnp.abs(flow_ref[1, k])) + top_sound for k in range(3)
    ]
    dcols = [by_sublane(DMAT[:, j], 8) for j in range(N)]
    def load_state(a, carry):
        for v in range(V):
            for b in range(N):
                u_ref[pl.ds(tile(v, a, b), N), :] = state_ref[v, a, b]
        return carry

    def pack_halo(ref):
        for v in range(V):
            left = jnp.zeros((N, LANES), f32)
            right = jnp.zeros((N, LANES), f32)
            for a in range(N):
                left = jnp.where(slot6 == a, roll(ref[face(v, a, 0), :], a), left)
                right = jnp.where(slot6 == a, roll(ref[face(v, a, N - 1), :], a - EA + 1), right)
            west_out[v, pl.ds(0, N), :] = left
            east_out[v, pl.ds(0, N), :] = right

    def pack_trace(read):
        quarter = lane6 // SLAB
        turned = jnp.where(is_rotor, (quarter + 1) % 4, quarter)
        for t in range(8):
            merged = jnp.zeros((N, LANES), f32)
            for q in range(4):
                n = 4 * t + q
                if n < V * N:
                    here = read(n // N, n % N)
                    merged = jnp.where(turned == q, roll(here, SLAB * q), merged)
            trace_out[pl.ds(N * t, N), :] = jnp.where(is_rotor, roll(merged, SLAB), merged)

    def copy(section, k, src, dst, target):
        return pltpu.make_async_remote_copy(
            src_ref=src,
            dst_ref=dst,
            send_sem=send_sem.at[section, k],
            recv_sem=recv_sem.at[section, k],
            device_id=target,
            device_id_type=MESH,
        )

    def send_across(section):
        copies = [
            copy(section, 2 + h, trace_out, hop_in.at[section, h], across(h))
            for h in sorted(range(groups), key=lambda h: -min(h, groups - h))
        ]
        for c in copies:
            c.start()
        return copies

    def send_halos(section):
        copies = [
            copy(section, 0, west_out, west_in.at[section], around(-1)),
            copy(section, 1, east_out, east_in.at[section], around(1)),
        ]
        for c in copies:
            c.start()
        return copies

    def send_within(section):
        amount = jnp.where(
            is_rotor,
            lax.rem(2 * sectors - offset_ref[section] - 1, sectors),
            lax.rem(offset_ref[section], sectors),
        )
        high, low = amount // group, lax.rem(amount, group)
        arrived = [hop_in[section, h] for h in range(groups)]
        facing = choose(lax.rem(high + (member + low) // group, groups), arrived)
        prior = choose(lax.rem(high + (member + low + 1) // group, groups), arrived)
        copies = []
        for g in sorted(range(1, group), key=lambda g: -min(g, group - g)):
            pair_out[g - 1] = jnp.where(low == g, facing, prior)
            copies.append(
                copy(
                    section,
                    1 + groups + g,
                    pair_out.at[g - 1],
                    pair_in.at[section, g],
                    within(g),
                )
            )
            copies[-1].start()
        pair_in[section, 0] = jnp.where(low == 0, facing, prior)
        return copies, low

    def volume(src, dst, base, scale):
        k1 = -scale * s1 * speed[0]
        c1 = -scale * s1 * sound
        k2 = jnp.full((8, LANES), -2.0 * scale * speed[1], f32)
        k3 = jnp.full((8, LANES), -2.0 * scale * speed[2], f32)
        c2 = jnp.full((8, LANES), -2.0 * scale * sound, f32)

        def at_b(b, carry):
            row_b = [choose(b, [f32(DMAT[k, j]) for k in range(N)]) for j in range(N)]
            for a in range(N):
                kept = {}
                zero_sum = None
                for v in range(V):
                    start = tile(v, a, b)
                    g1 = dcols[0] * src[pl.ds(start, 1), :]
                    for j in range(1, N):
                        g1 = g1 + dcols[j] * src[pl.ds(start + j, 1), :]
                    g2 = row_b[0] * get(src, v, a, 0)
                    for j in range(1, N):
                        g2 = g2 + row_b[j] * get(src, v, a, j)
                    g3 = None
                    for j in range(N):
                        if j != a:
                            term = f32(DMAT[a, j]) * get(src, v, j, b)
                            g3 = term if g3 is None else g3 + term
                    total = base(v, a, b) + k1 * g1 + k2 * g2 + k3 * g3
                    if v == 0:
                        kept = {1: g1, 2: g2, 3: g3}
                        zero_sum = total
                        continue
                    if v == 1:
                        total = total + c1 * kept[1]
                        zero_sum = zero_sum + c1 * g1
                    if v == 2:
                        total = total + c2 * kept[2]
                        zero_sum = zero_sum + c2 * g2
                    if v == 3:
                        total = total + c2 * kept[3]
                        zero_sum = zero_sum + c2 * g3
                    dst[pl.ds(start, 8), :] = total
                dst[pl.ds(tile(0, a, b), 8), :] = zero_sum
            return carry

        lax.fori_loop(0, N, at_b, 0)

    def jumps(outside, inside, direction, sign, factor, along, acoustic):
        result = []
        for v in range(V):
            flux = along * outside[v]
            if v == 0:
                flux = flux + acoustic * outside[direction]
            if v == direction:
                flux = flux + acoustic * outside[0]
            gap = outside[v] if inside is None else outside[v] - inside[v]
            result.append(factor * (sign * flux + spread[direction - 1] * gap))
        return result

    def inner_faces(src, dst, scale):
        def azimuthal(a, carry):
            lows = [src[face(v, a, 0), :] for v in range(V)]
            highs = [src[face(v, a, N - 1), :] for v in range(V)]
            before = [jnp.where(slot6 == 0, 0.0, roll(x, 1)) for x in highs]
            after = [jnp.where(slot6 == EA - 1, 0.0, roll(x, -1)) for x in lows]
            factor = scale * HALF * s1_6
            for c, out, ins, sign in ((0, before, lows, 1.0), (N - 1, after, highs, -1.0)):
                for v, x in enumerate(jumps(out, ins, 1, sign, factor, speed[0], sound)):
                    dst[face(v, a, c), :] = dst[face(v, a, c), :] + x
            return carry

        lax.fori_loop(0, N, azimuthal, 0)

        def radial_faces(a, carry):
            lows = [get(src, v, a, 0) for v in range(V)]
            highs = [get(src, v, a, N - 1) for v in range(V)]
            below = [
                jnp.where(radial == 0, -lows[v] if v == 2 else lows[v], roll(highs[v], EA))
                for v in range(V)
            ]
            above = [
                jnp.where(radial == ER - 1, -highs[v] if v == 2 else highs[v], roll(lows[v], -EA))
                for v in range(V)
            ]
            factor = scale * LIFT
            for b, out, ins, sign in ((0, below, lows, 1.0), (N - 1, above, highs, -1.0)):
                for v, x in enumerate(jumps(out, ins, 2, sign, factor, speed[1], sound)):
                    dst[pl.ds(tile(v, a, b), 8), :] = get(dst, v, a, b) + x
            return carry

        lax.fori_loop(0, N, radial_faces, 0)

        def axial_faces(b, carry):
            lows = [get(src, v, 0, b) for v in range(V)]
            highs = [get(src, v, N - 1, b) for v in range(V)]
            below = [jnp.where(lane < SLAB, 0.0, roll(x, SLAB)) for x in highs]
            above = [jnp.where(lane >= LANES - SLAB, 0.0, roll(x, -SLAB)) for x in lows]
            factor = scale * LIFT
            for a, out, ins, sign in ((0, below, lows, 1.0), (N - 1, above, highs, -1.0)):
                for v, x in enumerate(jumps(out, ins, 3, sign, factor, speed[2], sound)):
                    dst[pl.ds(tile(v, a, b), 8), :] = get(dst, v, a, b) + x
            return carry

        lax.fori_loop(0, N, axial_faces, 0)

    def halo_faces(section, dst, scale):
        factor = scale * HALF * s1_6
        from_west = [east_in[section, v, pl.ds(0, N), :] for v in range(V)]
        from_east = [west_in[section, v, pl.ds(0, N), :] for v in range(V)]
        low = jumps(from_west, None, 1, 1.0, factor, speed[0], sound)
        high = jumps(from_east, None, 1, -1.0, factor, speed[0], sound)
        for v in range(V):
            for a in range(N):
                x = jnp.where(slot6 == 0, roll(low[v], -a), 0.0)
                dst[face(v, a, 0), :] = dst[face(v, a, 0), :] + x
                x = jnp.where(slot6 == EA - 1, roll(high[v], EA - 1 - a), 0.0)
                dst[face(v, a, N - 1), :] = dst[face(v, a, N - 1), :] + x

    def mortar(section):
        whole = lax.rem(frac_ref[section] // FRACS, EA)
        fraction = lax.rem(frac_ref[section], FRACS).astype(f32) / FRACS
        start = jnp.where(is_rotor, whole, EA - 1 - whole)
        scaled = by_sublane((POINTS + 1.0) / 2.0, N)
        rotor_up = jnp.where(scaled + fraction >= 1.0, 1.0, 0.0)
        stator_up = jnp.where(scaled > fraction, 1.0, 0.0)
        upper = jnp.where(is_rotor, rotor_up, stator_up)
        signed = jnp.where(is_rotor, scaled + fraction, scaled - fraction)
        base = jnp.where(is_rotor, 0.0, 1.0)
        local = (signed + base - upper) * 2.0 - 1.0
        weights = []
        for source in range(N):
            weight = jnp.ones_like(local)
            for another in range(N):
                if another != source:
                    weight = weight * (
                        (local - f32(POINTS[another]))
                        * f32(1.0 / (POINTS[source] - POINTS[another]))
                    )
            weights.append(weight)
        return upper, weights, start

    def interface(section, digit, tables, dst, scale):
        upper, weights, start = tables
        packed = []
        for t in range(8):
            held = [pair_in[section, g, pl.ds(N * t, N), :] for g in range(group)]
            first = choose(digit, held[1:] + held[:1])
            second = choose(digit, held)
            lower = jnp.where(slot6 < EA - start, turn(first, -start), turn(second, EA - start))
            after = jnp.where(
                slot6 < EA - 1 - start, turn(first, -start - 1), turn(second, EA - 1 - start)
            )
            value = None
            for s in range(N):
                here = jnp.where(upper > 0.5, after[s : s + 1], lower[s : s + 1])
                value = weights[s] * here if value is None else value + weights[s] * here
            packed.append(value)
        begin = jnp.where(is_rotor, LANES - SLAB, 0)
        valid = (lane6 >= begin) & (lane6 < begin + SLAB)
        sign = jnp.where(is_rotor, -1.0, 1.0)
        for b in range(N):
            outside = []
            for v in range(V):
                n = v * N + b
                outside.append(jnp.where(valid, turn(packed[n // 4], begin - SLAB * (n % 4)), 0.0))
            terms = jumps(outside, None, 3, sign, scale * LIFT, other_axial, other_sound)
            for v in range(V):
                rows = pl.ds(tile(v, own_a, b), N)
                dst[rows, :] = dst[rows, :] + terms[v]

    def run_section(section, first, src, dst, base, scale, early):
        pack_halo(src)
        halos = send_halos(section)
        volume(src, dst, base, scale)
        inner_faces(src, dst, scale)
        tables = mortar(section)
        for c in first:
            c.wait()
        last, digit = send_within(section)
        for c in halos:
            c.wait()
        halo_faces(section, dst, scale)
        early()
        for c in last:
            c.wait()
        interface(section, digit, tables, dst, scale)

    def store_layer(a, carry):
        for v in range(V):
            for b in range(N):
                out_ref[v, a, b] = u_ref[pl.ds(tile(v, a, b), N), :]
        return carry

    loads[0].wait()
    pack_trace(lambda v, b: face_ref[v, b])
    pl.semaphore_wait(barrier, len(partners))
    first = send_across(0)
    loads[4].wait()
    lax.fori_loop(0, N, load_state, 0)
    run_section(0, first, u_ref, w_ref, lambda v, a, b: get(u_ref, v, a, b), TIME_STEP, lambda: None)
    pack_trace(lambda v, b: w_ref[pl.ds(tile(v, own_a, b), N), :])
    run_section(
        1,
        send_across(1),
        w_ref,
        u_ref,
        lambda v, a, b: 0.5 * (get(u_ref, v, a, b) + get(w_ref, v, a, b)),
        0.5 * TIME_STEP,
        lambda: lax.fori_loop(0, N, store_layer, 0),
    )
    store_layer(own_a, 0)


def solution(mesh):
    sectors = mesh.shape["sector"]
    group, groups = split_cycle(sectors)
    n_sems = 1 + groups + group

    def per_device(state, mean_flow, sector_offset, frac_index):
        hbm = pl.BlockSpec(memory_space=pltpu.HBM)
        vmem = pl.BlockSpec(memory_space=pltpu.VMEM)
        rows = V * N * N * 8
        return pl.pallas_call(
            functools.partial(kernel, sectors),
            out_shape=pltpu.VMEM(state.shape, f32),
            in_specs=[hbm, hbm, hbm, hbm],
            out_specs=vmem,
            scratch_shapes=[
                pltpu.SMEM(mean_flow.shape, f32),
                pltpu.SMEM(sector_offset.shape, jnp.int32),
                pltpu.SMEM(frac_index.shape, jnp.int32),
                pltpu.VMEM(state.shape, f32),
                pltpu.VMEM((V, N, N, LANES), f32),
                pltpu.VMEM((rows, LANES), f32),
                pltpu.VMEM((rows, LANES), f32),
                pltpu.VMEM((V, 8, LANES), f32),
                pltpu.VMEM((V, 8, LANES), f32),
                pltpu.VMEM((2, V, 8, LANES), f32),
                pltpu.VMEM((2, V, 8, LANES), f32),
                pltpu.VMEM((TRACE_ROWS, LANES), f32),
                pltpu.VMEM((2, groups, TRACE_ROWS, LANES), f32),
                pltpu.VMEM((max(group - 1, 1), TRACE_ROWS, LANES), f32),
                pltpu.VMEM((2, group, TRACE_ROWS, LANES), f32),
                pltpu.SemaphoreType.DMA((5,)),
                pltpu.SemaphoreType.DMA((2, n_sems)),
                pltpu.SemaphoreType.DMA((2, n_sems)),
            ],
            compiler_params=pltpu.CompilerParams(collective_id=0, has_side_effects=True),
        )(mean_flow, sector_offset, frac_index, state)

    spec = P(None, None, None, None, ("blk", "sector"))
    return jax.shard_map(
        per_device, mesh=mesh, in_specs=(spec, P(), P(), P()), out_specs=spec, check_vma=False
    )
```
